128 devices in a mesh: front: 4 (over y), blk: 32 (over z, x, core).
Axes of the slice: x: 4, y: 4, z: 4, core: 2. Of those that a mesh axis runs over, the one named last changes fastest.
Arguments:
- front_matrix: float32 [4, 13312, 13312], P('front', 'blk')
- random_probe: float32 [4, 13312, 256], P('front', 'blk'), may hold values from -6 to 6
- child_samples: float32 [4, 12288, 256], P('front', 'blk'), may hold values from -6 to 6
- child_dest: int32 [4, 12288], P('front', 'blk'), may hold values from 0 to 13311, as said below
- skeleton: int32 [4, 32, 128], P('front', 'blk'), may hold values from 0 to 415, as said below
- leaf_ranks: int32 [4, 32], P('front', 'blk'), may hold values from 64 to 128, as said below
- pair_skeleton: int32 [4, 16, 128], P('front'), may hold values from 0 to 255, as said below
Outputs:
- interp_leaf: float32 [4, 13312, 128], P('front', 'blk')
- interp_pair: float32 [4, 4096, 128], P('front', 'blk')
The draws below stay inside these ranges and needn't reach their ends.
Inputs may be any that keep to these rules, and one draw needn't show every extreme that they name: `child_dest`: among the rows of one device, at most 24 name rows of one leaf node; in every group one leaf node of the next group receives exactly 24 rows from every device of the group. `skeleton`: the 128 entries of one leaf are distinct. `leaf_ranks`: 128 is reached in every front. `pair_skeleton`: the 128 entries of one node are distinct and name live slots only: k of leaf 2q with k below its rank, or 128 + k of leaf 2q+1 with k below its rank.
All inputs are finite; a program needn't handle non-finite values.
Results may differ from the reference program's by a relative error of at most 0.0003.
Values sent between devices are 32-bit elements; how exact they have to be, the bound alone decides.
No kernel may reach another device: no remote copies, remote signals or barrier semaphores. Data moves between devices by JAX's collectives and lax.ppermute only.
A program may use at most 192 MiB of HBM per device.

```python
import math
import jax
import jax.numpy as jnp
from jax import lax

NF = 13312
SMP = 256
RMAX = 128
RMIN = 64
R2 = 128
CR_DEV = 384
P_DEV = 416
CHROWS = 12288
CAP = 24
N_FRONT = 4
N_BLK = 32


def draw_front_matrix(key, part):
    front_keys = jax.random.split(key, N_FRONT)

    def one_front(front_key):
        noise_key, diag_key = jax.random.split(front_key, 2)
        base_noise = jax.random.normal(noise_key, (NF, NF), jnp.float32)
        coupling = (base_noise + base_noise.T) * (2.0 * NF) ** (-0.5)
        diagonal = jnp.exp(jax.random.uniform(diag_key, (NF,), jnp.float32, 0.0, math.log(4.0)))
        positions = jnp.arange(NF)
        return coupling.at[positions, positions].add(diagonal)
    return lax.map(one_front, front_keys)


def draw_child_dest(key, part):

    def one_group(group_key):
        heavy_block = jax.random.randint(jax.random.fold_in(group_key, 0), (), 0, N_BLK)
        block_keys = jax.random.split(jax.random.fold_in(group_key, 1), N_BLK)

        def one_block(block_key):
            score_key, order_key, spot_key = jax.random.split(block_key, 3)
            slot_ids = jnp.arange(N_BLK * CAP, dtype=jnp.int32)
            scores = jax.random.randint(score_key, (N_BLK * CAP,), 1, 2 ** 30)
            scores = jnp.where(slot_ids // CAP == heavy_block, 0, scores)
            taken_slots = jnp.argsort(scores, stable=True)[:CR_DEV].astype(jnp.int32)
            device = jax.random.permutation(order_key, taken_slots // CAP)
            within = jax.random.randint(spot_key, (CR_DEV,), 0, P_DEV)
            return (device * P_DEV + within).astype(jnp.int32)
        return lax.map(one_block, block_keys).reshape(N_BLK * CR_DEV)
    return lax.map(one_group, jax.random.split(key, N_FRONT))


def draw_skeleton(key, part):
    leaf_keys = jax.random.split(jax.random.fold_in(key, 5), N_FRONT * N_BLK)
    pick_rows = jax.vmap(lambda leaf_key: jax.random.permutation(leaf_key, P_DEV)[:RMAX])(leaf_keys)
    return pick_rows.reshape(N_FRONT, N_BLK, RMAX).astype(jnp.int32)


def rank_table(key):
    table_key = jax.random.fold_in(key, 11)
    drawn_ranks = jax.random.randint(jax.random.fold_in(table_key, 1), (N_FRONT, N_BLK), RMIN, RMAX + 1)
    fullest = jax.random.randint(jax.random.fold_in(table_key, 2), (N_FRONT, 1), 0, N_BLK)
    return jnp.where(jnp.arange(N_BLK)[None, :] == fullest, RMAX, drawn_ranks).astype(jnp.int32)


def draw_leaf_ranks(key, part):
    return rank_table(key)


def draw_pair_skeleton(key, part):
    rank_grid = rank_table(key)
    paired = rank_grid.reshape(N_FRONT, N_BLK // 2, 2)
    slot_ids = jnp.arange(2 * RMAX, dtype=jnp.int32)
    live_slots = jnp.where(slot_ids < RMAX, slot_ids < paired[..., 0:1], slot_ids - RMAX < paired[..., 1:2])
    scores = jax.random.randint(jax.random.fold_in(key, 23), (N_FRONT, N_BLK // 2, 2 * RMAX), 1, 2 ** 30)
    scores = jnp.where(live_slots, scores, 2 ** 30)
    return jnp.argsort(scores, axis=-1, stable=True)[..., :R2].astype(jnp.int32)


def levels(key, dims, pieces, smallest, top_value):
    factor_of, own = 1.0, jax.random.fold_in(key, 6)
    for position, parts in pieces:
        steps = jnp.exp(jax.random.uniform(jax.random.fold_in(own, position), (parts,), jnp.float32, smallest / len(pieces), top_value / len(pieces)))
        factor_of = factor_of * jnp.repeat(steps, dims[position] // parts).reshape([-1 if axis == position else 1 for axis in range(len(dims))])
    return factor_of


def scatter_about(key, shape, width, most, pieces=(), held_as=jnp.bfloat16):
    drawn = jax.random.normal(key, shape, jnp.float32) * width
    if len(pieces) > 0:
        drawn = levels(key, shape, pieces, -0.22, 0.18) * drawn
    return jnp.clip(drawn, min=-most, max=most).astype(held_as)


def setup_inputs(seed: int = 0) -> dict:
    seeds = jax.random.split(jax.random.key(seed), 8)
    front_matrix = draw_front_matrix(jax.random.fold_in(seeds[7], 71), 0)
    random_probe = scatter_about(seeds[1], (N_FRONT, NF, SMP), 1.0, 6.0, ((0, 4), (1, 32)), jnp.float32)
    child_samples = scatter_about(seeds[2], (N_FRONT, CHROWS, SMP), 1.0, 6.0, ((0, 4), (1, 32)), jnp.float32)
    child_dest = draw_child_dest(jax.random.fold_in(seeds[7], 71), 0)
    skeleton = draw_skeleton(jax.random.fold_in(seeds[7], 71), 0)
    leaf_ranks = draw_leaf_ranks(jax.random.fold_in(seeds[7], 71), 0)
    pair_skeleton = draw_pair_skeleton(jax.random.fold_in(seeds[7], 71), 0)
    return dict(front_matrix=front_matrix, random_probe=random_probe, child_samples=child_samples, child_dest=child_dest, skeleton=skeleton, leaf_ranks=leaf_ranks, pair_skeleton=pair_skeleton)


HIGHEST = lax.Precision.HIGHEST
ridge_share = 0.1

def exact_dot(left, right):
    return jnp.dot(left.astype(jnp.float32), right.astype(jnp.float32), precision=HIGHEST, preferred_element_type=jnp.float32)

def interpolate(targets, leaf_basis, live_mask, live_count):
    gram_matrix = exact_dot(leaf_basis, leaf_basis.T)
    ridge_size = ridge_share * jnp.sum(jnp.diagonal(gram_matrix)) / live_count
    gram_matrix = gram_matrix + jnp.diag(jnp.where(live_mask, ridge_size, 1.0))
    factor = jnp.linalg.cholesky(gram_matrix)
    cross_terms = exact_dot(targets, leaf_basis.T)
    return jax.scipy.linalg.cho_solve((factor, True), cross_terms.T).T

def leaf_terms(matrix, probe_all, sample, leaf_index, chosen, leaf_rank):
    height = NF // N_BLK
    start_row = leaf_index * height
    row_block = lax.dynamic_slice_in_dim(matrix, start_row, height, 0)
    diagonal_block = lax.dynamic_slice_in_dim(row_block, start_row, height, 1)
    own_probe = lax.dynamic_slice_in_dim(probe_all, start_row, height, 0)
    local_sample = lax.dynamic_slice_in_dim(sample, start_row, height, 0)
    off_sample = local_sample - exact_dot(diagonal_block, own_probe)
    live_mask = jnp.arange(RMAX) < leaf_rank
    leaf_basis = off_sample[chosen] * live_mask[:, None]
    leaf_interp = interpolate(off_sample, leaf_basis, live_mask, leaf_rank.astype(jnp.float32))
    pair_start = leaf_index // 2 * (2 * height)
    pair_columns = lax.dynamic_slice_in_dim(row_block, pair_start, 2 * height, 1)[chosen]
    pair_probe = lax.dynamic_slice_in_dim(probe_all, pair_start, 2 * height, 0)
    upward = (local_sample[chosen] - exact_dot(pair_columns, pair_probe)) * live_mask[:, None]
    return (leaf_interp, upward)

def reference(front_matrix, random_probe, child_samples, child_dest, skeleton, leaf_ranks, pair_skeleton):
    leaf_parts = []
    pair_parts = []
    for front_index in range(N_FRONT):
        source = (front_index - 1) % N_FRONT
        matrix = front_matrix[front_index]
        probe_all = random_probe[front_index]
        sample = exact_dot(matrix, probe_all) + jax.ops.segment_sum(child_samples[source], child_dest[source], num_segments=NF)

        def one_leaf(inputs):
            leaf_index, chosen, leaf_rank = inputs
            return leaf_terms(matrix, probe_all, sample, leaf_index, chosen, leaf_rank)
        leaf_interp, upward = lax.map(one_leaf, (jnp.arange(N_BLK, dtype=jnp.int32), skeleton[front_index], leaf_ranks[front_index]))
        stacked = upward.reshape(N_BLK // 2, 2 * RMAX, SMP)

        def one_pair(inputs):
            targets, pick_rows = inputs
            return interpolate(targets, targets[pick_rows], jnp.ones((R2,), jnp.bool_), float(R2))
        pair_interp = lax.map(one_pair, (stacked, pair_skeleton[front_index]))
        leaf_parts.append(leaf_interp.reshape(NF, RMAX))
        pair_parts.append(pair_interp.reshape(N_BLK * RMAX, R2))
    return (jnp.stack(leaf_parts), jnp.stack(pair_parts))
```

```python
import jax
import jax.numpy as jnp
from jax import lax
from jax.experimental import pallas as pl
from jax.experimental.pallas import tpu as pltpu
from jax.sharding import Mesh
from jax.sharding import PartitionSpec as P


BLK = ("blk_0", "blk_1", "blk_2")

f32, bf16 = jnp.float32, jnp.bfloat16
HIGHEST = lax.Precision.HIGHEST
ridge_share = 0.1
HEIGHT, SAMPLES, RANK = 416, 256, 128
CAP, WIDE, GROUP = 24, 512, 56

TREE = (
    ((1, 0), (0, 0), "p", 1),
    ((3, 0), (0, 0), "p", -1),
    ((0, 1), (0, 0), "q", 1),
    ((0, 3), (0, 0), "q", -1),
    ((2, 0), (1, 0), "p", 1),
    ((1, 3), (1, 0), "q", -1),
    ((3, 1), (3, 0), "q", 1),
    ((1, 1), (1, 0), "q", 1),
    ((3, 3), (3, 0), "q", -1),
    ((3, 2), (3, 1), "q", 1),
    ((1, 2), (1, 3), "q", -1),
    ((0, 2), (0, 1), "q", 1),
    ((2, 3), (2, 0), "q", -1),
    ((2, 2), (3, 2), "p", -1),
    ((2, 1), (2, 0), "q", 1),
)
GROUPS = (
    ((1, 0), (3, 0)),
    ((0, 1), (0, 3), (2, 0)),
    ((1, 3), (3, 1), (1, 1)),
    ((3, 3), (3, 2), (1, 2)),
    ((0, 2), (2, 3)),
    ((2, 2), (2, 1)),
)


def chips_step(value, kind, step):
    def at(z, x, c):
        return ((z % 4) * 4 + x % 4) * 2 + c

    pairs = []
    for z in range(4):
        for x in range(4):
            for c in range(2):
                along_x = (kind == "p") == (c == 0)
                pairs.append((at(z, x, c), at(z, x + step, c) if along_x else at(z + step, x, c)))
    return lax.ppermute(value, BLK, pairs)


def swap_cores(value):
    return lax.ppermute(value, "blk_2", [(0, 1), (1, 0)])


def split2(x):
    hi = x.astype(bf16)
    return hi, (x - hi.astype(f32)).astype(bf16)


def split3(x):
    hi = x.astype(bf16)
    rest = x - hi.astype(f32)
    mid = rest.astype(bf16)
    return hi, mid, (rest - mid.astype(f32)).astype(bf16)


def mxu(a, b, dims):
    return lax.dot_general(a, b, (dims, ((), ())), preferred_element_type=f32)


NN, NT, TN = ((1,), (0,)), ((1,), (1,)), ((0,), (0,))


def dot3(a, b, dims):
    ah, al = split2(a)
    bh, bl = split2(b)
    return mxu(al, bh, dims) + mxu(ah, bl, dims) + mxu(ah, bh, dims)


def pack_kernel(rows_ref, dest_ref, out_ref):
    count = rows_ref.shape[0]
    dest = dest_ref[...].astype(f32)
    leaf_id = lax.broadcasted_iota(jnp.int32, (32, count), 0).astype(f32)
    low = leaf_id * float(HEIGHT)
    member = ((dest >= low) & (dest < low + float(HEIGHT))).astype(f32)
    earlier = lax.broadcasted_iota(jnp.int32, (count, count), 0) < lax.broadcasted_iota(
        jnp.int32, (count, count), 1
    )
    before = mxu(member.astype(bf16), earlier.astype(f32).astype(bf16), NN)
    place = jnp.sum(member * before, axis=0, keepdims=True)
    leaf = jnp.sum(member * leaf_id, axis=0, keepdims=True)
    chip = jnp.floor(leaf * 0.5)
    within = dest - leaf * float(HEIGHT)
    slot = (leaf - 2.0 * chip) * float(CAP) + place
    where = (chip * float(GROUP) + slot).astype(jnp.int32)
    total = 16 * GROUP
    chosen = lax.broadcasted_iota(jnp.int32, (total, count), 0) == where
    chosen = chosen.astype(f32).astype(bf16)
    hi, lo = split2(rows_ref[...])
    out_ref[...] = mxu(chosen, hi, NN) + mxu(chosen, lo, NN)
    chip_id = lax.broadcasted_iota(jnp.int32, (16, count), 0).astype(f32)
    lane_id = lax.broadcasted_iota(jnp.int32, (128, count), 0).astype(f32)
    labels = lax.dot_general(
        jnp.where(chip == chip_id, within, 0.0),
        (slot == lane_id).astype(f32),
        (NT, ((), ())),
        precision=HIGHEST,
        preferred_element_type=f32,
    )
    for j in range(16):
        out_ref[j * GROUP + 2 * CAP : j * GROUP + 2 * CAP + 1, 0:128] = labels[j : j + 1, :]


def pack(rows, dest):
    return pl.pallas_call(
        pack_kernel,
        out_shape=jax.ShapeDtypeStruct((16 * GROUP, SAMPLES), f32),
        compiler_params=pltpu.CompilerParams(vmem_limit_bytes=24 * 1024 * 1024),
        cost_estimate=pl.CostEstimate(flops=400_000_000, bytes_accessed=2_000_000, transcendentals=0),
    )(rows, dest)


def unpack_kernel(where_ref, in_ref, mine_ref, other_ref, label_ref):
    label_ref[...] = jnp.zeros_like(label_ref)
    for j in range(16):
        label_ref[j : j + 1, :] = in_ref[j, 2 * CAP : 2 * CAP + 1, 0:128]
    labels = label_ref[...].T
    row_id = lax.broadcasted_iota(jnp.int32, (CAP, HEIGHT), 1).astype(f32)
    sums = []
    for half in range(2):
        lo_row = half * CAP
        picks = jnp.concatenate(
            [(labels[lo_row : lo_row + CAP, j : j + 1] == row_id).astype(f32) for j in range(16)],
            axis=0,
        ).astype(bf16)
        rows = in_ref[:, lo_row : lo_row + CAP, :].reshape(16 * CAP, SAMPLES)
        hi, lo = split2(rows)
        sums.append(mxu(picks, hi, TN) + mxu(picks, lo, TN))
    first = where_ref[2] == 0
    mine_ref[...] = jnp.where(first, sums[0], sums[1])
    other_ref[...] = jnp.where(first, sums[1], sums[0])


def unpack(where, arrived):
    half = jax.ShapeDtypeStruct((HEIGHT, SAMPLES), f32)
    vmem = pl.BlockSpec(memory_space=pltpu.VMEM)
    return pl.pallas_call(
        unpack_kernel,
        out_shape=(half, half),
        in_specs=[pl.BlockSpec(memory_space=pltpu.SMEM), vmem],
        out_specs=(vmem, vmem),
        scratch_shapes=[pltpu.VMEM((128, 128), f32)],
        compiler_params=pltpu.CompilerParams(vmem_limit_bytes=24 * 1024 * 1024),
        cost_estimate=pl.CostEstimate(flops=400_000_000, bytes_accessed=2_000_000, transcendentals=0),
    )(where, arrived)


def leaf_of(where_ref, block, sibling):
    z, x, c = where_ref[0], where_ref[1], where_ref[2]
    p, q = block
    if sibling:
        c = 1 - c
    first = c == 0
    from_z = lax.rem(z + 4 - jnp.where(first, q, p), 4)
    from_x = lax.rem(x + 4 - jnp.where(first, p, q), 4)
    return (from_z * 4 + from_x) * 2 + c


def product_kernel(blocks, first, last, *refs):
    refs = list(refs)
    where_ref, rank_ref, matrix_ref = refs[:3]
    refs = refs[3:]
    probes, refs = refs[: len(blocks)], refs[len(blocks) :]
    if first:
        out_ref, near_ref, wide, high, low, sem = refs
    elif last:
        total_ref, mine_ref, other_ref, chosen_ref, out_ref, up_ref, wide, high, low, sem = refs
    else:
        total_ref, out_ref, wide, high, low, sem = refs
    leaves = [leaf_of(where_ref, *b) for b in blocks]
    copies = []
    for k, leaf in enumerate(leaves):
        start = pl.multiple_of((leaf * 13) // 4 * 128, 128)
        copies.append(
            pltpu.make_async_copy(matrix_ref.at[:, pl.ds(start, WIDE)], wide.at[k], sem.at[k])
        )
        copies[-1].start()
    total = None if first else total_ref[...]
    for k, leaf in enumerate(leaves):
        slot = k % 2
        for hold in (high, low):
            hold[slot, 0:96, :] = jnp.zeros((96, SAMPLES), bf16)
            hold[slot, HEIGHT:WIDE, :] = jnp.zeros((96, SAMPLES), bf16)
        copies[k].wait()
        offset = pl.multiple_of(lax.rem(leaf, 4) * 32, 32)
        hi, lo = split2(probes[k][...])
        high[slot, pl.ds(offset, HEIGHT), :] = hi
        low[slot, pl.ds(offset, HEIGHT), :] = lo
        xh, xl = high[slot], low[slot]
        parts = []
        for rows in (slice(0, 208), slice(208, 416)):
            mh, ml = split2(wide[k, rows, :])
            left = jnp.concatenate([ml, mh, mh], axis=1)
            right = jnp.concatenate([xh, xl, xh], axis=0)
            parts.append(mxu(left, right, NN))
        term = jnp.concatenate(parts, axis=0)
        if first and k == 0:
            near_ref[...] = term
        else:
            total = term if total is None else total + term
    if last:
        total = total + (mine_ref[...] + other_ref[...])
        picks = pick_matrix(chosen_ref[...], HEIGHT)
        live = lax.broadcasted_iota(jnp.int32, (RANK, SAMPLES), 0) < rank_ref[0]
        up_ref[...] = jnp.where(live, take(picks, total), 0.0)
    out_ref[...] = total


def pick_matrix(row, width):
    column = jnp.broadcast_to(row.astype(f32), (RANK, RANK)).T
    parts = []
    for start in range(0, width, RANK):
        size = min(RANK, width - start)
        lane = lax.broadcasted_iota(jnp.int32, (RANK, size), 1).astype(f32) + float(start)
        parts.append((column[:, :size] == lane).astype(f32))
    return jnp.concatenate(parts, axis=1).astype(bf16)


def take(picks, values):
    hi, mid, lo = split3(values)
    return (mxu(picks, lo, NN) + mxu(picks, mid, NN)) + mxu(picks, hi, NN)


def product(where, rank, matrix, blocks, probes, total=None, last=None):
    count = len(blocks)
    smem = pl.BlockSpec(memory_space=pltpu.SMEM)
    vmem = pl.BlockSpec(memory_space=pltpu.VMEM)
    args = [where, rank, matrix, *probes]
    specs = [smem, smem, pl.BlockSpec(memory_space=pltpu.HBM)] + [vmem] * count
    out_shape = [jax.ShapeDtypeStruct((HEIGHT, SAMPLES), f32)]
    first = total is None
    if first:
        out_shape.append(jax.ShapeDtypeStruct((HEIGHT, SAMPLES), f32))
    else:
        args.append(total)
        specs.append(vmem)
    if last is not None:
        args += list(last)
        specs += [vmem] * len(last)
        out_shape.append(jax.ShapeDtypeStruct((RANK, SAMPLES), f32))

    def kernel(*refs):
        product_kernel(blocks, first, last is not None, *refs)

    out = pl.pallas_call(
        kernel,
        out_shape=tuple(out_shape),
        in_specs=specs,
        out_specs=tuple([vmem] * len(out_shape)),
        scratch_shapes=[
            pltpu.VMEM((count, HEIGHT, WIDE), f32),
            pltpu.VMEM((2, WIDE, SAMPLES), bf16),
            pltpu.VMEM((2, WIDE, SAMPLES), bf16),
            pltpu.SemaphoreType.DMA((count,)),
        ],
        compiler_params=pltpu.CompilerParams(vmem_limit_bytes=44 * 1024 * 1024),
        cost_estimate=pl.CostEstimate(
            flops=count * 6 * HEIGHT * WIDE * SAMPLES,
            bytes_accessed=count * 4 * HEIGHT * (WIDE + SAMPLES),
            transcendentals=0,
        ),
    )(*args)
    return out if len(out_shape) > 1 else out[0]


def total_of(terms):
    while len(terms) > 1:
        terms = [sum(terms[i + 1 : i + 2], terms[i]) for i in range(0, len(terms), 2)]
    return terms[0]


def small_inverse(s):
    n = len(s)
    if n == 2:
        r = 1.0 / (s[0][0] * s[1][1] - s[0][1] * s[0][1])
        off = -(s[0][1] * r)
        return [[s[1][1] * r, off], [off, s[0][0] * r]]
    h = n // 2
    span = range(h)
    b = [[s[i][h + j] for j in span] for i in span]
    p = small_inverse([[s[i][j] for j in span] for i in span])
    w = [[total_of([p[i][k] * b[k][j] for k in span]) for j in span] for i in span]
    rest = [[None] * h for _ in span]
    for i in span:
        for j in range(i, h):
            rest[i][j] = rest[j][i] = s[h + i][h + j] - total_of([b[k][i] * w[k][j] for k in span])
    q = small_inverse(rest)
    e = [[total_of([w[i][k] * q[k][j] for k in span]) for j in span] for i in span]
    out = [[None] * n for _ in range(n)]
    for i in span:
        for j in span:
            out[i][h + j] = out[h + j][i] = -e[i][j]
            out[h + i][h + j] = q[i][j]
            if j >= i:
                out[i][j] = out[j][i] = p[i][j] + total_of([e[i][k] * w[j][k] for k in span])
    return out


def by_position(index, values):
    bit = 1
    while len(values) > 1:
        odd = (index & bit) != 0
        values = [jnp.where(odd, values[i + 1], values[i]) for i in range(0, len(values), 2)]
        bit *= 2
    return values[0]


def eliminate(panel, at, first):
    lane = lax.broadcasted_iota(jnp.int32, (8, RANK), 1)
    sub = lax.broadcasted_iota(jnp.int32, (8, RANK), 0)
    inside = (lane >= first) & (lane < first + 8)
    tile = panel[at]
    rows = [jnp.broadcast_to(tile[a : a + 1, :], (8, RANK)) for a in range(8)]
    s = [[None] * 8 for _ in range(8)]
    for a in range(8):
        for b in range(a, 8):
            s[a][b] = s[b][a] = jnp.broadcast_to(rows[a][:, first + b : first + b + 1], (8, RANK))
    d = small_inverse(s)
    scaled = []
    for a in range(8):
        own = by_position(lane, d[a])
        scaled.append(jnp.where(inside, own, total_of([d[a][b] * rows[b] for b in range(8)])))
    out = []
    for t, old in enumerate(panel):
        if t == at:
            out.append(by_position(sub, scaled))
            continue
        columns = [jnp.broadcast_to(old[:, first + a : first + a + 1], (8, RANK)) for a in range(8)]
        out.append(jnp.where(inside, 0.0, old) - total_of([c * r for c, r in zip(columns, scaled)]))
    return out


def invert(refs, tiles=8):
    lane = lax.broadcasted_iota(jnp.int32, (RANK, RANK), 1)
    row = lax.broadcasted_iota(jnp.int32, (RANK, RANK), 0)
    height = 8 * tiles
    for start in range(0, RANK, height):
        panels = [[ref[start + 8 * t : start + 8 * t + 8, :] for t in range(tiles)] for ref in refs]
        for t in range(tiles):
            panels = [eliminate(panel, t, start + 8 * t) for panel in panels]
        for ref, panel in zip(refs, panels):
            old = ref[...]
            inside = (lane >= start) & (lane < start + height)
            new = jnp.concatenate(panel, axis=0)
            zeros = lambda n: [jnp.zeros((n, RANK), f32)] if n else []
            full = jnp.concatenate(zeros(start) + [new] + zeros(RANK - start - height), axis=0)
            ch, cm, cl = split3(jnp.where(inside, old, 0.0))
            rh, rm, rl = split3(full)
            change = mxu(
                jnp.concatenate([cl, cm, ch, cm, ch, ch], axis=1),
                jnp.concatenate([rh, rm, rl, rh, rm, rh], axis=0),
                NN,
            )
            in_panel = (row >= start) & (row < start + height)
            ref[...] = jnp.where(in_panel, full, jnp.where(inside, 0.0, old) - change)


def system_of(basis, live, count):
    gram = dot3(basis, basis, NT)
    ridge = ridge_share * jnp.sum(basis * basis, keepdims=True) / count
    i = lax.broadcasted_iota(jnp.int32, (RANK, RANK), 0)
    j = lax.broadcasted_iota(jnp.int32, (RANK, RANK), 1)
    shift = jnp.broadcast_to(ridge, (RANK, RANK))
    if live is not None:
        shift = jnp.where(i < live, shift, 1.0)
    return gram + jnp.where(i == j, shift, 0.0)


def finish_kernel(
    where_ref, rank_ref, sum_ref, near_ref, up_ref, sibling_ref, chosen_ref, pick_ref, leaf_ref, pair_ref, hold
):
    rank = rank_ref[0]
    off = sum_ref[...] + near_ref[...]
    live = lax.broadcasted_iota(jnp.int32, (RANK, SAMPLES), 0) < rank
    basis = jnp.where(live, take(pick_matrix(chosen_ref[...], HEIGHT), off), 0.0)
    up = up_ref[...]
    pick = pick_ref[...]
    pick = jnp.where(where_ref[2] == 0, pick, (pick + RANK) & (2 * RANK - 1))
    picks = pick_matrix(pick, 2 * RANK)
    pair_basis = take(picks[:, :RANK], up) + take(picks[:, RANK:], sibling_ref[...])
    hold[0] = system_of(basis, rank, rank.astype(f32))
    hold[1] = system_of(pair_basis, None, float(RANK))
    leaf_cross = dot3(off, basis, NT)
    pair_cross = dot3(up, pair_basis, NT)
    invert([hold.at[0], hold.at[1]])
    leaf_ref[...] = dot3(leaf_cross, hold[0], NN)
    pair_ref[...] = dot3(pair_cross, hold[1], NN)


def finish(where, rank, total, near, upward, sibling, chosen, pick):
    smem = pl.BlockSpec(memory_space=pltpu.SMEM)
    vmem = pl.BlockSpec(memory_space=pltpu.VMEM)
    return pl.pallas_call(
        finish_kernel,
        out_shape=(
            jax.ShapeDtypeStruct((HEIGHT, RANK), f32),
            jax.ShapeDtypeStruct((RANK, RANK), f32),
        ),
        in_specs=[smem, smem] + [vmem] * 6,
        out_specs=(vmem, vmem),
        scratch_shapes=[pltpu.VMEM((2, RANK, RANK), f32)],
        compiler_params=pltpu.CompilerParams(vmem_limit_bytes=24 * 1024 * 1024),
        cost_estimate=pl.CostEstimate(flops=2_000_000_000, bytes_accessed=2_000_000, transcendentals=0),
    )(where, rank, total, near, upward, sibling, chosen, pick)


def body(
    front_matrix, random_probe, child_samples, child_dest, skeleton, leaf_ranks, pair_skeleton
):
    matrix, own = front_matrix[0], random_probe[0]
    z, x, c = lax.axis_index("blk_0"), lax.axis_index("blk_1"), lax.axis_index("blk_2")
    where = jnp.stack([z, x, c]).astype(jnp.int32)
    rank = leaf_ranks[0]
    chosen = skeleton[0]
    pick = lax.dynamic_slice_in_dim(pair_skeleton[0], z * 4 + x, 1, 0)

    ahead = [(k, (k + 1) % 4) for k in range(4)]
    got = {(0, 0): own}
    for arrives, sent, kind, step in TREE:
        got[arrives] = chips_step(got[sent], kind, step)
    rows = lax.ppermute(child_samples[0], "front", ahead)
    dest = lax.ppermute(child_dest, "front", ahead)
    sending = pack(rows, dest).reshape(16, GROUP, SAMPLES)
    arrived = lax.all_to_all(sending, ("blk_0", "blk_1"), 0, 0, tiled=True)
    mine, other = unpack(where, arrived)
    other = swap_cores(other)
    near_probe = swap_cores(own)
    total = near = None
    for n, group in enumerate(GROUPS):
        blocks = [(b, s) for s in (False, True) for b in group]
        probes = [got[b] for b in group] + [swap_cores(got[b]) for b in group]
        if n == 0:
            blocks, probes = [((0, 0), True)] + blocks, [near_probe] + probes
        last = (mine, other, chosen) if n == len(GROUPS) - 1 else None
        total = product(where, rank, matrix, blocks, probes, total, last)
        if n == 0:
            total, near = total
    total, upward = total
    sibling = swap_cores(upward)
    leaf_interp, pair_interp = finish(where, rank, total, near, upward, sibling, chosen, pick)
    return (leaf_interp[None], pair_interp[None])


def solution(mesh):
    torus = Mesh(
        mesh.devices.reshape(mesh.shape["front"], 4, 4, 2), ("front", "blk_0", "blk_1", "blk_2")
    )
    return jax.shard_map(
        body,
        mesh=torus,
        in_specs=(
            P("front", BLK, None),
            P("front", BLK, None),
            P("front", BLK, None),
            P("front", BLK),
            P("front", BLK, None),
            P("front", BLK),
            P("front", None, None),
        ),
        out_specs=(P("front", BLK, None), P("front", BLK, None)),
        check_vma=False,
    )
```

```python
import jax
import jax.numpy as jnp
from jax import lax
from jax.experimental import pallas as pl
from jax.experimental.pallas import tpu as pltpu
from jax.sharding import Mesh
from jax.sharding import PartitionSpec as P


BLK = ("blk_0", "blk_1", "blk_2")

f32, bf16 = jnp.float32, jnp.bfloat16
HIGHEST = lax.Precision.HIGHEST
ridge_share = 0.1
HEIGHT, SAMPLES, RANK = 416, 256, 128
CAP, WIDE, GROUP = 24, 512, 56

TREE = (
    ((1, 0), (0, 0), "p", 1),
    ((3, 0), (0, 0), "p", -1),
    ((0, 1), (0, 0), "q", 1),
    ((0, 3), (0, 0), "q", -1),
    ((2, 0), (1, 0), "p", 1),
    ((1, 3), (1, 0), "q", -1),
    ((3, 1), (3, 0), "q", 1),
    ((1, 1), (1, 0), "q", 1),
    ((3, 3), (3, 0), "q", -1),
    ((3, 2), (3, 1), "q", 1),
    ((1, 2), (1, 3), "q", -1),
    ((0, 2), (0, 1), "q", 1),
    ((2, 3), (2, 0), "q", -1),
    ((2, 2), (3, 2), "p", -1),
    ((2, 1), (2, 0), "q", 1),
)
GROUPS = (
    ((1, 0), (3, 0)),
    ((0, 1), (0, 3), (2, 0)),
    ((1, 3), (3, 1), (1, 1)),
    ((3, 3), (3, 2), (1, 2), (0, 2), (2, 3)),
    ((2, 2), (2, 1)),
)


def chips_step(value, kind, step):
    def at(z, x, c):
        return ((z % 4) * 4 + x % 4) * 2 + c

    pairs = []
    for z in range(4):
        for x in range(4):
            for c in range(2):
                along_x = (kind == "p") == (c == 0)
                pairs.append((at(z, x, c), at(z, x + step, c) if along_x else at(z + step, x, c)))
    return lax.ppermute(value, BLK, pairs)


def swap_cores(value):
    return lax.ppermute(value, "blk_2", [(0, 1), (1, 0)])


def split2(x):
    hi = x.astype(bf16)
    return hi, (x - hi.astype(f32)).astype(bf16)


def split3(x):
    hi = x.astype(bf16)
    rest = x - hi.astype(f32)
    mid = rest.astype(bf16)
    return hi, mid, (rest - mid.astype(f32)).astype(bf16)


def mxu(a, b, dims):
    return lax.dot_general(a, b, (dims, ((), ())), preferred_element_type=f32)


NN, NT, TN = ((1,), (0,)), ((1,), (1,)), ((0,), (0,))


def dot3(a, b, dims):
    ah, al = split2(a)
    bh, bl = split2(b)
    return mxu(al, bh, dims) + mxu(ah, bl, dims) + mxu(ah, bh, dims)


def pack_kernel(rows_ref, dest_ref, out_ref):
    count = rows_ref.shape[0]
    dest = dest_ref[...].astype(f32)
    leaf_id = lax.broadcasted_iota(jnp.int32, (32, count), 0).astype(f32)
    low = leaf_id * float(HEIGHT)
    member = ((dest >= low) & (dest < low + float(HEIGHT))).astype(f32)
    earlier = lax.broadcasted_iota(jnp.int32, (count, count), 0) < lax.broadcasted_iota(
        jnp.int32, (count, count), 1
    )
    before = mxu(member.astype(bf16), earlier.astype(f32).astype(bf16), NN)
    place = jnp.sum(member * before, axis=0, keepdims=True)
    leaf = jnp.sum(member * leaf_id, axis=0, keepdims=True)
    chip = jnp.floor(leaf * 0.5)
    within = dest - leaf * float(HEIGHT)
    slot = (leaf - 2.0 * chip) * float(CAP) + place
    where = (chip * float(GROUP) + slot).astype(jnp.int32)
    total = 16 * GROUP
    chosen = lax.broadcasted_iota(jnp.int32, (total, count), 0) == where
    chosen = chosen.astype(f32).astype(bf16)
    hi, lo = split2(rows_ref[...])
    out_ref[...] = mxu(chosen, hi, NN) + mxu(chosen, lo, NN)
    chip_id = lax.broadcasted_iota(jnp.int32, (16, count), 0).astype(f32)
    lane_id = lax.broadcasted_iota(jnp.int32, (128, count), 0).astype(f32)
    labels = lax.dot_general(
        jnp.where(chip == chip_id, within, 0.0),
        (slot == lane_id).astype(f32),
        (NT, ((), ())),
        precision=HIGHEST,
        preferred_element_type=f32,
    )
    for j in range(16):
        out_ref[j * GROUP + 2 * CAP : j * GROUP + 2 * CAP + 1, 0:128] = labels[j : j + 1, :]


def pack(rows, dest):
    return pl.pallas_call(
        pack_kernel,
        out_shape=jax.ShapeDtypeStruct((16 * GROUP, SAMPLES), f32),
        compiler_params=pltpu.CompilerParams(vmem_limit_bytes=12 * 1024 * 1024),
        cost_estimate=pl.CostEstimate(flops=400_000_000, bytes_accessed=2_000_000, transcendentals=0),
    )(rows, dest)


def unpack_kernel(where_ref, in_ref, mine_ref, other_ref, label_ref):
    label_ref[...] = jnp.zeros_like(label_ref)
    for j in range(16):
        label_ref[j : j + 1, :] = in_ref[j, 2 * CAP : 2 * CAP + 1, 0:128]
    labels = label_ref[...].T
    row_id = lax.broadcasted_iota(jnp.int32, (CAP, HEIGHT), 1).astype(f32)
    sums = []
    for half in range(2):
        lo_row = half * CAP
        picks = jnp.concatenate(
            [(labels[lo_row : lo_row + CAP, j : j + 1] == row_id).astype(f32) for j in range(16)],
            axis=0,
        ).astype(bf16)
        rows = in_ref[:, lo_row : lo_row + CAP, :].reshape(16 * CAP, SAMPLES)
        hi, lo = split2(rows)
        sums.append(mxu(picks, hi, TN) + mxu(picks, lo, TN))
    first = where_ref[2] == 0
    mine_ref[...] = jnp.where(first, sums[0], sums[1])
    other_ref[...] = jnp.where(first, sums[1], sums[0])


def unpack(where, arrived):
    half = jax.ShapeDtypeStruct((HEIGHT, SAMPLES), f32)
    vmem = pl.BlockSpec(memory_space=pltpu.VMEM)
    return pl.pallas_call(
        unpack_kernel,
        out_shape=(half, half),
        in_specs=[pl.BlockSpec(memory_space=pltpu.SMEM), vmem],
        out_specs=(vmem, vmem),
        scratch_shapes=[pltpu.VMEM((128, 128), f32)],
        compiler_params=pltpu.CompilerParams(vmem_limit_bytes=12 * 1024 * 1024),
        cost_estimate=pl.CostEstimate(flops=400_000_000, bytes_accessed=2_000_000, transcendentals=0),
    )(where, arrived)


def leaf_of(where_ref, block, sibling):
    z, x, c = where_ref[0], where_ref[1], where_ref[2]
    p, q = block
    if sibling:
        c = 1 - c
    first = c == 0
    from_z = lax.rem(z + 4 - jnp.where(first, q, p), 4)
    from_x = lax.rem(x + 4 - jnp.where(first, p, q), 4)
    return (from_z * 4 + from_x) * 2 + c


def product_kernel(blocks, first, last, *refs):
    refs = list(refs)
    where_ref, rank_ref, matrix_ref = refs[:3]
    refs = refs[3:]
    probes, refs = refs[: len(blocks)], refs[len(blocks) :]
    if first:
        out_ref, near_ref, wide, high, low, sem = refs
    elif last:
        total_ref, mine_ref, other_ref, chosen_ref, out_ref, up_ref, wide, high, low, sem = refs
    else:
        total_ref, out_ref, wide, high, low, sem = refs
    leaves = [leaf_of(where_ref, *b) for b in blocks]
    copies = []
    for k, leaf in enumerate(leaves):
        start = pl.multiple_of((leaf * 13) // 4 * 128, 128)
        copies.append(
            pltpu.make_async_copy(matrix_ref.at[:, pl.ds(start, WIDE)], wide.at[k], sem.at[k])
        )
        copies[-1].start()
    total = None if first else total_ref[...]
    for k, leaf in enumerate(leaves):
        slot = k % 2
        for hold in (high, low):
            hold[slot, 0:96, :] = jnp.zeros((96, SAMPLES), bf16)
            hold[slot, HEIGHT:WIDE, :] = jnp.zeros((96, SAMPLES), bf16)
        copies[k].wait()
        offset = pl.multiple_of(lax.rem(leaf, 4) * 32, 32)
        hi, lo = split2(probes[k][...])
        high[slot, pl.ds(offset, HEIGHT), :] = hi
        low[slot, pl.ds(offset, HEIGHT), :] = lo
        xh, xl = high[slot], low[slot]
        parts = []
        for rows in (slice(0, 208), slice(208, 416)):
            mh, ml = split2(wide[k, rows, :])
            left = jnp.concatenate([ml, mh, mh], axis=1)
            right = jnp.concatenate([xh, xl, xh], axis=0)
            parts.append(mxu(left, right, NN))
        term = jnp.concatenate(parts, axis=0)
        if first and k == 0:
            near_ref[...] = term
        else:
            total = term if total is None else total + term
    if last:
        total = total + (mine_ref[...] + other_ref[...])
        picks = pick_matrix(chosen_ref[...], HEIGHT)
        live = lax.broadcasted_iota(jnp.int32, (RANK, SAMPLES), 0) < rank_ref[0]
        up_ref[...] = jnp.where(live, take(picks, total), 0.0)
    out_ref[...] = total


def pick_matrix(row, width):
    column = jnp.broadcast_to(row.astype(f32), (RANK, RANK)).T
    parts = []
    for start in range(0, width, RANK):
        size = min(RANK, width - start)
        lane = lax.broadcasted_iota(jnp.int32, (RANK, size), 1).astype(f32) + float(start)
        parts.append((column[:, :size] == lane).astype(f32))
    return jnp.concatenate(parts, axis=1).astype(bf16)


def take(picks, values):
    hi, mid, lo = split3(values)
    return (mxu(picks, lo, NN) + mxu(picks, mid, NN)) + mxu(picks, hi, NN)


def product(where, rank, matrix, blocks, probes, total=None, last=None):
    count = len(blocks)
    smem = pl.BlockSpec(memory_space=pltpu.SMEM)
    vmem = pl.BlockSpec(memory_space=pltpu.VMEM)
    args = [where, rank, matrix, *probes]
    specs = [smem, smem, pl.BlockSpec(memory_space=pltpu.HBM)] + [vmem] * count
    out_shape = [jax.ShapeDtypeStruct((HEIGHT, SAMPLES), f32)]
    first = total is None
    if first:
        out_shape.append(jax.ShapeDtypeStruct((HEIGHT, SAMPLES), f32))
    else:
        args.append(total)
        specs.append(vmem)
    if last is not None:
        args += list(last)
        specs += [vmem] * len(last)
        out_shape.append(jax.ShapeDtypeStruct((RANK, SAMPLES), f32))

    def kernel(*refs):
        product_kernel(blocks, first, last is not None, *refs)

    out = pl.pallas_call(
        kernel,
        out_shape=tuple(out_shape),
        in_specs=specs,
        out_specs=tuple([vmem] * len(out_shape)),
        scratch_shapes=[
            pltpu.VMEM((count, HEIGHT, WIDE), f32),
            pltpu.VMEM((2, WIDE, SAMPLES), bf16),
            pltpu.VMEM((2, WIDE, SAMPLES), bf16),
            pltpu.SemaphoreType.DMA((count,)),
        ],
        compiler_params=pltpu.CompilerParams(vmem_limit_bytes=44 * 1024 * 1024),
        cost_estimate=pl.CostEstimate(
            flops=count * 6 * HEIGHT * WIDE * SAMPLES,
            bytes_accessed=count * 4 * HEIGHT * (WIDE + SAMPLES),
            transcendentals=0,
        ),
    )(*args)
    return out if len(out_shape) > 1 else out[0]


def total_of(terms):
    while len(terms) > 1:
        terms = [sum(terms[i + 1 : i + 2], terms[i]) for i in range(0, len(terms), 2)]
    return terms[0]


def small_inverse(s):
    n = len(s)
    if n == 2:
        r = 1.0 / (s[0][0] * s[1][1] - s[0][1] * s[0][1])
        off = -(s[0][1] * r)
        return [[s[1][1] * r, off], [off, s[0][0] * r]]
    h = n // 2
    span = range(h)
    b = [[s[i][h + j] for j in span] for i in span]
    p = small_inverse([[s[i][j] for j in span] for i in span])
    w = [[total_of([p[i][k] * b[k][j] for k in span]) for j in span] for i in span]
    rest = [[None] * h for _ in span]
    for i in span:
        for j in range(i, h):
            rest[i][j] = rest[j][i] = s[h + i][h + j] - total_of([b[k][i] * w[k][j] for k in span])
    q = small_inverse(rest)
    e = [[total_of([w[i][k] * q[k][j] for k in span]) for j in span] for i in span]
    out = [[None] * n for _ in range(n)]
    for i in span:
        for j in span:
            out[i][h + j] = out[h + j][i] = -e[i][j]
            out[h + i][h + j] = q[i][j]
            if j >= i:
                out[i][j] = out[j][i] = p[i][j] + total_of([e[i][k] * w[j][k] for k in span])
    return out


def by_position(index, values):
    bit = 1
    while len(values) > 1:
        odd = (index & bit) != 0
        values = [jnp.where(odd, values[i + 1], values[i]) for i in range(0, len(values), 2)]
        bit *= 2
    return values[0]


def eliminate(panel, at, first):
    lane = lax.broadcasted_iota(jnp.int32, (8, RANK), 1)
    sub = lax.broadcasted_iota(jnp.int32, (8, RANK), 0)
    inside = (lane >= first) & (lane < first + 8)
    tile = panel[at]
    rows = [jnp.broadcast_to(tile[a : a + 1, :], (8, RANK)) for a in range(8)]
    s = [[None] * 8 for _ in range(8)]
    for a in range(8):
        for b in range(a, 8):
            s[a][b] = s[b][a] = jnp.broadcast_to(rows[a][:, first + b : first + b + 1], (8, RANK))
    d = small_inverse(s)
    scaled = []
    for a in range(8):
        own = by_position(lane, d[a])
        scaled.append(jnp.where(inside, own, total_of([d[a][b] * rows[b] for b in range(8)])))
    out = []
    for t, old in enumerate(panel):
        if t == at:
            out.append(by_position(sub, scaled))
            continue
        columns = [jnp.broadcast_to(old[:, first + a : first + a + 1], (8, RANK)) for a in range(8)]
        out.append(jnp.where(inside, 0.0, old) - total_of([c * r for c, r in zip(columns, scaled)]))
    return out


def invert(refs, tiles=8):
    lane = lax.broadcasted_iota(jnp.int32, (RANK, RANK), 1)
    row = lax.broadcasted_iota(jnp.int32, (RANK, RANK), 0)
    height = 8 * tiles
    for start in range(0, RANK, height):
        panels = [[ref[start + 8 * t : start + 8 * t + 8, :] for t in range(tiles)] for ref in refs]
        for t in range(tiles):
            panels = [eliminate(panel, t, start + 8 * t) for panel in panels]
        for ref, panel in zip(refs, panels):
            old = ref[...]
            inside = (lane >= start) & (lane < start + height)
            new = jnp.concatenate(panel, axis=0)
            zeros = lambda n: [jnp.zeros((n, RANK), f32)] if n else []
            full = jnp.concatenate(zeros(start) + [new] + zeros(RANK - start - height), axis=0)
            ch, cm, cl = split3(jnp.where(inside, old, 0.0))
            rh, rm, rl = split3(full)
            change = mxu(
                jnp.concatenate([cl, cm, ch, cm, ch, ch], axis=1),
                jnp.concatenate([rh, rm, rl, rh, rm, rh], axis=0),
                NN,
            )
            in_panel = (row >= start) & (row < start + height)
            ref[...] = jnp.where(in_panel, full, jnp.where(inside, 0.0, old) - change)


def system_of(basis, live, count):
    gram = dot3(basis, basis, NT)
    ridge = ridge_share * jnp.sum(basis * basis, keepdims=True) / count
    i = lax.broadcasted_iota(jnp.int32, (RANK, RANK), 0)
    j = lax.broadcasted_iota(jnp.int32, (RANK, RANK), 1)
    shift = jnp.broadcast_to(ridge, (RANK, RANK))
    if live is not None:
        shift = jnp.where(i < live, shift, 1.0)
    return gram + jnp.where(i == j, shift, 0.0)


def finish_kernel(
    where_ref, rank_ref, sum_ref, near_ref, up_ref, sibling_ref, chosen_ref, pick_ref, leaf_ref, pair_ref, hold
):
    rank = rank_ref[0]
    off = sum_ref[...] + near_ref[...]
    live = lax.broadcasted_iota(jnp.int32, (RANK, SAMPLES), 0) < rank
    basis = jnp.where(live, take(pick_matrix(chosen_ref[...], HEIGHT), off), 0.0)
    up = up_ref[...]
    pick = pick_ref[...]
    pick = jnp.where(where_ref[2] == 0, pick, (pick + RANK) & (2 * RANK - 1))
    picks = pick_matrix(pick, 2 * RANK)
    pair_basis = take(picks[:, :RANK], up) + take(picks[:, RANK:], sibling_ref[...])
    hold[0] = system_of(basis, rank, rank.astype(f32))
    hold[1] = system_of(pair_basis, None, float(RANK))
    leaf_cross = dot3(off, basis, NT)
    pair_cross = dot3(up, pair_basis, NT)
    invert([hold.at[0], hold.at[1]])
    leaf_ref[...] = dot3(leaf_cross, hold[0], NN)
    pair_ref[...] = dot3(pair_cross, hold[1], NN)


def finish(where, rank, total, near, upward, sibling, chosen, pick):
    smem = pl.BlockSpec(memory_space=pltpu.SMEM)
    vmem = pl.BlockSpec(memory_space=pltpu.VMEM)
    return pl.pallas_call(
        finish_kernel,
        out_shape=(
            jax.ShapeDtypeStruct((HEIGHT, RANK), f32),
            jax.ShapeDtypeStruct((RANK, RANK), f32),
        ),
        in_specs=[smem, smem] + [vmem] * 6,
        out_specs=(vmem, vmem),
        scratch_shapes=[pltpu.VMEM((2, RANK, RANK), f32)],
        compiler_params=pltpu.CompilerParams(vmem_limit_bytes=12 * 1024 * 1024),
        cost_estimate=pl.CostEstimate(flops=2_000_000_000, bytes_accessed=2_000_000, transcendentals=0),
    )(where, rank, total, near, upward, sibling, chosen, pick)


def body(
    front_matrix, random_probe, child_samples, child_dest, skeleton, leaf_ranks, pair_skeleton
):
    matrix, own = front_matrix[0], random_probe[0]
    z, x, c = lax.axis_index("blk_0"), lax.axis_index("blk_1"), lax.axis_index("blk_2")
    where = jnp.stack([z, x, c]).astype(jnp.int32)
    rank = leaf_ranks[0]
    chosen = skeleton[0]
    pick = lax.dynamic_slice_in_dim(pair_skeleton[0], z * 4 + x, 1, 0)

    ahead = [(k, (k + 1) % 4) for k in range(4)]
    got = {(0, 0): own}
    for arrives, sent, kind, step in TREE:
        got[arrives] = chips_step(got[sent], kind, step)
    rows = lax.ppermute(child_samples[0], "front", ahead)
    dest = lax.ppermute(child_dest, "front", ahead)
    sending = pack(rows, dest).reshape(16, GROUP, SAMPLES)
    arrived = lax.all_to_all(sending, ("blk_0", "blk_1"), 0, 0, tiled=True)
    mine, other = unpack(where, arrived)
    other = swap_cores(other)
    near_probe = swap_cores(own)
    total = near = None
    for n, group in enumerate(GROUPS):
        blocks = [(b, s) for s in (False, True) for b in group]
        probes = [got[b] for b in group] + [swap_cores(got[b]) for b in group]
        if n == 0:
            blocks, probes = [((0, 0), True)] + blocks, [near_probe] + probes
        last = (mine, other, chosen) if n == len(GROUPS) - 1 else None
        total = product(where, rank, matrix, blocks, probes, total, last)
        if n == 0:
            total, near = total
    total, upward = total
    sibling = swap_cores(upward)
    leaf_interp, pair_interp = finish(where, rank, total, near, upward, sibling, chosen, pick)
    return (leaf_interp[None], pair_interp[None])


def solution(mesh):
    torus = Mesh(
        mesh.devices.reshape(mesh.shape["front"], 4, 4, 2), ("front", "blk_0", "blk_1", "blk_2")
    )
    return jax.shard_map(
        body,
        mesh=torus,
        in_specs=(
            P("front", BLK, None),
            P("front", BLK, None),
            P("front", BLK, None),
            P("front", BLK),
            P("front", BLK, None),
            P("front", BLK),
            P("front", None, None),
        ),
        out_specs=(P("front", BLK, None), P("front", BLK, None)),
        check_vma=False,
    )
```

```python
import jax
import jax.numpy as jnp
from jax import lax
from jax.experimental import pallas as pl
from jax.experimental.pallas import tpu as pltpu
from jax.sharding import Mesh
from jax.sharding import PartitionSpec as P


BLK = ("blk_0", "blk_1", "blk_2")

f32, bf16 = jnp.float32, jnp.bfloat16
HIGHEST = lax.Precision.HIGHEST
ridge_share = 0.1
HEIGHT, SAMPLES, RANK = 416, 256, 128
CAP, WIDE, GROUP = 24, 512, 56

TREE = (
    ((1, 0), (0, 0), "p", 1),
    ((3, 0), (0, 0), "p", -1),
    ((0, 1), (0, 0), "q", 1),
    ((0, 3), (0, 0), "q", -1),
    ((2, 0), (1, 0), "p", 1),
    ((1, 3), (1, 0), "q", -1),
    ((3, 1), (3, 0), "q", 1),
    ((1, 1), (1, 0), "q", 1),
    ((3, 3), (3, 0), "q", -1),
    ((3, 2), (3, 1), "q", 1),
    ((1, 2), (1, 3), "q", -1),
    ((0, 2), (0, 1), "q", 1),
    ((2, 3), (2, 0), "q", -1),
    ((2, 2), (3, 2), "p", -1),
    ((2, 1), (2, 0), "q", 1),
)
GROUPS = (
    ((1, 0), (3, 0)),
    ((0, 1), (0, 3), (2, 0)),
    ((1, 3), (3, 1), (1, 1)),
    ((3, 3), (3, 2), (1, 2), (0, 2), (2, 3)),
    ((2, 2), (2, 1)),
)


def chips_step(value, kind, step):
    def at(z, x, c):
        return ((z % 4) * 4 + x % 4) * 2 + c

    pairs = []
    for z in range(4):
        for x in range(4):
            for c in range(2):
                along_x = (kind == "p") == (c == 0)
                pairs.append((at(z, x, c), at(z, x + step, c) if along_x else at(z + step, x, c)))
    return lax.ppermute(value, BLK, pairs)


def swap_cores(value):
    return lax.ppermute(value, "blk_2", [(0, 1), (1, 0)])


def split2(x):
    hi = x.astype(bf16)
    return hi, (x - hi.astype(f32)).astype(bf16)


def split3(x):
    hi = x.astype(bf16)
    rest = x - hi.astype(f32)
    mid = rest.astype(bf16)
    return hi, mid, (rest - mid.astype(f32)).astype(bf16)


def mxu(a, b, dims):
    return lax.dot_general(a, b, (dims, ((), ())), preferred_element_type=f32)


NN, NT, TN = ((1,), (0,)), ((1,), (1,)), ((0,), (0,))


def dot3(a, b, dims):
    ah, al = split2(a)
    bh, bl = split2(b)
    return mxu(al, bh, dims) + mxu(ah, bl, dims) + mxu(ah, bh, dims)


def pack_kernel(rows_ref, dest_ref, out_ref):
    count = rows_ref.shape[0]
    dest = dest_ref[...].astype(f32)
    leaf_id = lax.broadcasted_iota(jnp.int32, (32, count), 0).astype(f32)
    low = leaf_id * float(HEIGHT)
    member = ((dest >= low) & (dest < low + float(HEIGHT))).astype(f32)
    earlier = lax.broadcasted_iota(jnp.int32, (count, count), 0) < lax.broadcasted_iota(
        jnp.int32, (count, count), 1
    )
    before = mxu(member.astype(bf16), earlier.astype(f32).astype(bf16), NN)
    place = jnp.sum(member * before, axis=0, keepdims=True)
    leaf = jnp.sum(member * leaf_id, axis=0, keepdims=True)
    chip = jnp.floor(leaf * 0.5)
    within = dest - leaf * float(HEIGHT)
    slot = (leaf - 2.0 * chip) * float(CAP) + place
    where = (chip * float(GROUP) + slot).astype(jnp.int32)
    total = 16 * GROUP
    chosen = lax.broadcasted_iota(jnp.int32, (total, count), 0) == where
    chosen = chosen.astype(f32).astype(bf16)
    hi, lo = split2(rows_ref[...])
    out_ref[...] = mxu(chosen, hi, NN) + mxu(chosen, lo, NN)
    chip_id = lax.broadcasted_iota(jnp.int32, (16, count), 0).astype(f32)
    lane_id = lax.broadcasted_iota(jnp.int32, (128, count), 0).astype(f32)
    labels = lax.dot_general(
        jnp.where(chip == chip_id, within, 0.0),
        (slot == lane_id).astype(f32),
        (NT, ((), ())),
        precision=HIGHEST,
        preferred_element_type=f32,
    )
    for j in range(16):
        out_ref[j * GROUP + 2 * CAP : j * GROUP + 2 * CAP + 1, 0:128] = labels[j : j + 1, :]


def pack(rows, dest):
    return pl.pallas_call(
        pack_kernel,
        out_shape=jax.ShapeDtypeStruct((16 * GROUP, SAMPLES), f32),
        compiler_params=pltpu.CompilerParams(vmem_limit_bytes=12 * 1024 * 1024),
        cost_estimate=pl.CostEstimate(flops=400_000_000, bytes_accessed=2_000_000, transcendentals=0),
    )(rows, dest)


def unpack_kernel(where_ref, in_ref, mine_ref, other_ref, label_ref):
    label_ref[...] = jnp.zeros_like(label_ref)
    for j in range(16):
        label_ref[j : j + 1, :] = in_ref[j, 2 * CAP : 2 * CAP + 1, 0:128]
    labels = label_ref[...].T
    row_id = lax.broadcasted_iota(jnp.int32, (CAP, HEIGHT), 1).astype(f32)
    sums = []
    for half in range(2):
        lo_row = half * CAP
        picks = jnp.concatenate(
            [(labels[lo_row : lo_row + CAP, j : j + 1] == row_id).astype(f32) for j in range(16)],
            axis=0,
        ).astype(bf16)
        rows = in_ref[:, lo_row : lo_row + CAP, :].reshape(16 * CAP, SAMPLES)
        hi, lo = split2(rows)
        sums.append(mxu(picks, hi, TN) + mxu(picks, lo, TN))
    first = where_ref[2] == 0
    mine_ref[...] = jnp.where(first, sums[0], sums[1])
    other_ref[...] = jnp.where(first, sums[1], sums[0])


def unpack(where, arrived):
    half = jax.ShapeDtypeStruct((HEIGHT, SAMPLES), f32)
    vmem = pl.BlockSpec(memory_space=pltpu.VMEM)
    return pl.pallas_call(
        unpack_kernel,
        out_shape=(half, half),
        in_specs=[pl.BlockSpec(memory_space=pltpu.SMEM), vmem],
        out_specs=(vmem, vmem),
        scratch_shapes=[pltpu.VMEM((128, 128), f32)],
        compiler_params=pltpu.CompilerParams(vmem_limit_bytes=12 * 1024 * 1024),
        cost_estimate=pl.CostEstimate(flops=400_000_000, bytes_accessed=2_000_000, transcendentals=0),
    )(where, arrived)


def leaf_of(where_ref, block, sibling):
    z, x, c = where_ref[0], where_ref[1], where_ref[2]
    p, q = block
    if sibling:
        c = 1 - c
    first = c == 0
    from_z = lax.rem(z + 4 - jnp.where(first, q, p), 4)
    from_x = lax.rem(x + 4 - jnp.where(first, p, q), 4)
    return (from_z * 4 + from_x) * 2 + c


def product_kernel(blocks, first, last, *refs):
    refs = list(refs)
    where_ref, rank_ref, matrix_ref = refs[:3]
    refs = refs[3:]
    probes, refs = refs[: len(blocks)], refs[len(blocks) :]
    if first:
        out_ref, near_ref, wide, high, low, sem = refs
    elif last:
        total_ref, mine_ref, other_ref, chosen_ref, out_ref, up_ref, wide, high, low, sem = refs
    else:
        total_ref, out_ref, wide, high, low, sem = refs
    leaves = [leaf_of(where_ref, *b) for b in blocks]
    copies = []
    for k, leaf in enumerate(leaves):
        start = pl.multiple_of((leaf * 13) // 4 * 128, 128)
        copies.append(
            pltpu.make_async_copy(matrix_ref.at[:, pl.ds(start, WIDE)], wide.at[k], sem.at[k])
        )
        copies[-1].start()
    total = None if first else total_ref[...]
    for k, leaf in enumerate(leaves):
        slot = k % 2
        for hold in (high, low):
            hold[slot, 0:96, :] = jnp.zeros((96, SAMPLES), bf16)
            hold[slot, HEIGHT:WIDE, :] = jnp.zeros((96, SAMPLES), bf16)
        copies[k].wait()
        offset = pl.multiple_of(lax.rem(leaf, 4) * 32, 32)
        hi, lo = split2(probes[k][...])
        high[slot, pl.ds(offset, HEIGHT), :] = hi
        low[slot, pl.ds(offset, HEIGHT), :] = lo
        xh, xl = high[slot], low[slot]
        parts = []
        for rows in (slice(0, 208), slice(208, 416)):
            mh, ml = split2(wide[k, rows, :])
            left = jnp.concatenate([ml, mh, mh], axis=1)
            right = jnp.concatenate([xh, xl, xh], axis=0)
            parts.append(mxu(left, right, NN))
        term = jnp.concatenate(parts, axis=0)
        if first and k == 0:
            near_ref[...] = term
        else:
            total = term if total is None else total + term
    if last:
        total = total + (mine_ref[...] + other_ref[...])
        picks = pick_matrix(chosen_ref[...], HEIGHT)
        live = lax.broadcasted_iota(jnp.int32, (RANK, SAMPLES), 0) < rank_ref[0]
        up_ref[...] = jnp.where(live, take(picks, total), 0.0)
    out_ref[...] = total


def pick_matrix(row, width):
    column = jnp.broadcast_to(row.astype(f32), (RANK, RANK)).T
    parts = []
    for start in range(0, width, RANK):
        size = min(RANK, width - start)
        lane = lax.broadcasted_iota(jnp.int32, (RANK, size), 1).astype(f32) + float(start)
        parts.append((column[:, :size] == lane).astype(f32))
    return jnp.concatenate(parts, axis=1).astype(bf16)


def take(picks, values):
    hi, mid, lo = split3(values)
    return (mxu(picks, lo, NN) + mxu(picks, mid, NN)) + mxu(picks, hi, NN)


def product(where, rank, matrix, blocks, probes, total=None, last=None):
    count = len(blocks)
    smem = pl.BlockSpec(memory_space=pltpu.SMEM)
    vmem = pl.BlockSpec(memory_space=pltpu.VMEM)
    args = [where, rank, matrix, *probes]
    specs = [smem, smem, pl.BlockSpec(memory_space=pltpu.HBM)] + [vmem] * count
    out_shape = [jax.ShapeDtypeStruct((HEIGHT, SAMPLES), f32)]
    first = total is None
    if first:
        out_shape.append(jax.ShapeDtypeStruct((HEIGHT, SAMPLES), f32))
    else:
        args.append(total)
        specs.append(vmem)
    if last is not None:
        args += list(last)
        specs += [vmem] * len(last)
        out_shape.append(jax.ShapeDtypeStruct((RANK, SAMPLES), f32))

    def kernel(*refs):
        product_kernel(blocks, first, last is not None, *refs)

    out = pl.pallas_call(
        kernel,
        out_shape=tuple(out_shape),
        in_specs=specs,
        out_specs=tuple([vmem] * len(out_shape)),
        scratch_shapes=[
            pltpu.VMEM((count, HEIGHT, WIDE), f32),
            pltpu.VMEM((2, WIDE, SAMPLES), bf16),
            pltpu.VMEM((2, WIDE, SAMPLES), bf16),
            pltpu.SemaphoreType.DMA((count,)),
        ],
        compiler_params=pltpu.CompilerParams(vmem_limit_bytes=44 * 1024 * 1024),
        cost_estimate=pl.CostEstimate(
            flops=count * 6 * HEIGHT * WIDE * SAMPLES,
            bytes_accessed=count * 4 * HEIGHT * (WIDE + SAMPLES),
            transcendentals=0,
        ),
    )(*args)
    return out if len(out_shape) > 1 else out[0]


def total_of(terms):
    while len(terms) > 1:
        terms = [sum(terms[i + 1 : i + 2], terms[i]) for i in range(0, len(terms), 2)]
    return terms[0]


def small_inverse(s):
    n = len(s)
    if n == 2:
        r = 1.0 / (s[0][0] * s[1][1] - s[0][1] * s[0][1])
        off = -(s[0][1] * r)
        return [[s[1][1] * r, off], [off, s[0][0] * r]]
    h = n // 2
    span = range(h)
    b = [[s[i][h + j] for j in span] for i in span]
    p = small_inverse([[s[i][j] for j in span] for i in span])
    w = [[total_of([p[i][k] * b[k][j] for k in span]) for j in span] for i in span]
    rest = [[None] * h for _ in span]
    for i in span:
        for j in range(i, h):
            rest[i][j] = rest[j][i] = s[h + i][h + j] - total_of([b[k][i] * w[k][j] for k in span])
    q = small_inverse(rest)
    e = [[total_of([w[i][k] * q[k][j] for k in span]) for j in span] for i in span]
    out = [[None] * n for _ in range(n)]
    for i in span:
        for j in span:
            out[i][h + j] = out[h + j][i] = -e[i][j]
            out[h + i][h + j] = q[i][j]
            if j >= i:
                out[i][j] = out[j][i] = p[i][j] + total_of([e[i][k] * w[j][k] for k in span])
    return out


def by_position(index, values):
    bit = 1
    while len(values) > 1:
        odd = (index & bit) != 0
        values = [jnp.where(odd, values[i + 1], values[i]) for i in range(0, len(values), 2)]
        bit *= 2
    return values[0]


def eliminate(panels, at, first):
    lane = lax.broadcasted_iota(jnp.int32, (8, RANK), 1)
    sub = lax.broadcasted_iota(jnp.int32, (8, RANK), 0)
    inside = (lane >= first) & (lane < first + 8)
    upper = sub < 4
    tiles = [panel[at] for panel in panels]
    rows = [jnp.where(upper, *(jnp.broadcast_to(t[a : a + 1, :], (8, RANK)) for t in tiles)) for a in range(8)]
    s = [[None] * 8 for _ in range(8)]
    for a in range(8):
        for b in range(a, 8):
            s[a][b] = s[b][a] = jnp.broadcast_to(rows[a][:, first + b : first + b + 1], (8, RANK))
    d = small_inverse(s)
    both = []
    for a in range(8):
        own = by_position(lane, d[a])
        both.append(jnp.where(inside, own, total_of([d[a][b] * rows[b] for b in range(8)])))
    results = []
    for panel, half in zip(panels, (0, 4)):
        scaled = [jnp.broadcast_to(v[half : half + 1, :], (8, RANK)) for v in both]
        out = []
        for t, old in enumerate(panel):
            if t == at:
                out.append(by_position(sub, scaled))
                continue
            columns = [jnp.broadcast_to(old[:, first + a : first + a + 1], (8, RANK)) for a in range(8)]
            out.append(jnp.where(inside, 0.0, old) - total_of([c * r for c, r in zip(columns, scaled)]))
        results.append(out)
    return results


def invert(refs, tiles=4):
    lane = lax.broadcasted_iota(jnp.int32, (RANK, RANK), 1)
    row = lax.broadcasted_iota(jnp.int32, (RANK, RANK), 0)
    height = 8 * tiles
    for start in range(0, RANK, height):
        panels = [[ref[start + 8 * t : start + 8 * t + 8, :] for t in range(tiles)] for ref in refs]
        for t in range(tiles):
            panels = eliminate(panels, t, start + 8 * t)
        for ref, panel in zip(refs, panels):
            old = ref[...]
            inside = (lane >= start) & (lane < start + height)
            new = jnp.concatenate(panel, axis=0)
            zeros = lambda n: [jnp.zeros((n, RANK), f32)] if n else []
            full = jnp.concatenate(zeros(start) + [new] + zeros(RANK - start - height), axis=0)
            ch, cm, cl = split3(jnp.where(inside, old, 0.0))
            rh, rm, rl = split3(full)
            change = mxu(
                jnp.concatenate([cl, cm, ch, cm, ch, ch], axis=1),
                jnp.concatenate([rh, rm, rl, rh, rm, rh], axis=0),
                NN,
            )
            in_panel = (row >= start) & (row < start + height)
            ref[...] = jnp.where(in_panel, full, jnp.where(inside, 0.0, old) - change)


def system_of(basis, live, count):
    gram = dot3(basis, basis, NT)
    ridge = ridge_share * jnp.sum(basis * basis, keepdims=True) / count
    i = lax.broadcasted_iota(jnp.int32, (RANK, RANK), 0)
    j = lax.broadcasted_iota(jnp.int32, (RANK, RANK), 1)
    shift = jnp.broadcast_to(ridge, (RANK, RANK))
    if live is not None:
        shift = jnp.where(i < live, shift, 1.0)
    return gram + jnp.where(i == j, shift, 0.0)


def finish_kernel(
    where_ref, rank_ref, sum_ref, near_ref, up_ref, sibling_ref, chosen_ref, pick_ref, leaf_ref, pair_ref, hold
):
    rank = rank_ref[0]
    off = sum_ref[...] + near_ref[...]
    live = lax.broadcasted_iota(jnp.int32, (RANK, SAMPLES), 0) < rank
    basis = jnp.where(live, take(pick_matrix(chosen_ref[...], HEIGHT), off), 0.0)
    up = up_ref[...]
    pick = pick_ref[...]
    pick = jnp.where(where_ref[2] == 0, pick, (pick + RANK) & (2 * RANK - 1))
    picks = pick_matrix(pick, 2 * RANK)
    pair_basis = take(picks[:, :RANK], up) + take(picks[:, RANK:], sibling_ref[...])
    hold[0] = system_of(basis, rank, rank.astype(f32))
    hold[1] = system_of(pair_basis, None, float(RANK))
    leaf_cross = dot3(off, basis, NT)
    pair_cross = dot3(up, pair_basis, NT)
    invert([hold.at[0], hold.at[1]])
    leaf_ref[...] = dot3(leaf_cross, hold[0], NN)
    pair_ref[...] = dot3(pair_cross, hold[1], NN)


def finish(where, rank, total, near, upward, sibling, chosen, pick):
    smem = pl.BlockSpec(memory_space=pltpu.SMEM)
    vmem = pl.BlockSpec(memory_space=pltpu.VMEM)
    return pl.pallas_call(
        finish_kernel,
        out_shape=(
            jax.ShapeDtypeStruct((HEIGHT, RANK), f32),
            jax.ShapeDtypeStruct((RANK, RANK), f32),
        ),
        in_specs=[smem, smem] + [vmem] * 6,
        out_specs=(vmem, vmem),
        scratch_shapes=[pltpu.VMEM((2, RANK, RANK), f32)],
        compiler_params=pltpu.CompilerParams(vmem_limit_bytes=12 * 1024 * 1024),
        cost_estimate=pl.CostEstimate(flops=2_000_000_000, bytes_accessed=2_000_000, transcendentals=0),
    )(where, rank, total, near, upward, sibling, chosen, pick)


def body(
    front_matrix, random_probe, child_samples, child_dest, skeleton, leaf_ranks, pair_skeleton
):
    matrix, own = front_matrix[0], random_probe[0]
    z, x, c = lax.axis_index("blk_0"), lax.axis_index("blk_1"), lax.axis_index("blk_2")
    where = jnp.stack([z, x, c]).astype(jnp.int32)
    rank = leaf_ranks[0]
    chosen = skeleton[0]
    pick = lax.dynamic_slice_in_dim(pair_skeleton[0], z * 4 + x, 1, 0)

    ahead = [(k, (k + 1) % 4) for k in range(4)]
    got = {(0, 0): own}
    for arrives, sent, kind, step in TREE:
        got[arrives] = chips_step(got[sent], kind, step)
    rows = lax.ppermute(child_samples[0], "front", ahead)
    dest = lax.ppermute(child_dest, "front", ahead)
    sending = pack(rows, dest).reshape(16, GROUP, SAMPLES)
    arrived = lax.all_to_all(sending, ("blk_0", "blk_1"), 0, 0, tiled=True)
    mine, other = unpack(where, arrived)
    other = swap_cores(other)
    near_probe = swap_cores(own)
    total = near = None
    for n, group in enumerate(GROUPS):
        blocks = [(b, s) for s in (False, True) for b in group]
        probes = [got[b] for b in group] + [swap_cores(got[b]) for b in group]
        if n == 0:
            blocks, probes = [((0, 0), True)] + blocks, [near_probe] + probes
        last = (mine, other, chosen) if n == len(GROUPS) - 1 else None
        total = product(where, rank, matrix, blocks, probes, total, last)
        if n == 0:
            total, near = total
    total, upward = total
    sibling = swap_cores(upward)
    leaf_interp, pair_interp = finish(where, rank, total, near, upward, sibling, chosen, pick)
    return (leaf_interp[None], pair_interp[None])


def solution(mesh):
    torus = Mesh(
        mesh.devices.reshape(mesh.shape["front"], 4, 4, 2), ("front", "blk_0", "blk_1", "blk_2")
    )
    return jax.shard_map(
        body,
        mesh=torus,
        in_specs=(
            P("front", BLK, None),
            P("front", BLK, None),
            P("front", BLK, None),
            P("front", BLK),
            P("front", BLK, None),
            P("front", BLK),
            P("front", None, None),
        ),
        out_specs=(P("front", BLK, None), P("front", BLK, None)),
        check_vma=False,
    )
```
